256 devices in a mesh: pipe: 8 (over x, core), bundle: 32 (over z, y).
Axes of the slice: x: 4, y: 4, z: 8, core: 2. Of those that a mesh axis runs over, the one named last changes fastest.
Arguments:
- act_fwd: bfloat16 [8, 2048, 8192], P('pipe', 'bundle'), may hold values from -6 to 6
- grad_in: bfloat16 [8, 2048, 8192], P('pipe', 'bundle'), may hold values from -6 to 6
- w_gate: bfloat16 [8, 8192, 4096], P('pipe', None, 'bundle'), may hold values from -0.0625 to 0.0625
- w_up: bfloat16 [8, 8192, 4096], P('pipe', None, 'bundle'), may hold values from -0.0625 to 0.0625
- w_down: bfloat16 [8, 4096, 8192], P('pipe', 'bundle'), may hold values from -0.09375 to 0.09375
- saved_gate: bfloat16 [8, 2048, 4096], P('pipe', None, 'bundle'), may hold values from -6 to 6
- saved_up: bfloat16 [8, 2048, 4096], P('pipe', None, 'bundle'), may hold values from -6 to 6
- mask_fwd: int32 [8, 128, 32], P('pipe'), may hold values from 0 to 1, as said below
- mask_bwd: int32 [8, 128, 32], P('pipe'), may hold values from 0 to 1, as said below
Outputs:
- next_forward: bfloat16 [8, 2048, 8192], P('pipe', 'bundle')
- next_backward: bfloat16 [8, 2048, 8192], P('pipe', 'bundle')
The draws below stay inside these ranges and needn't reach their ends.
Inputs may be any that keep to these rules, and one draw needn't show every extreme that they name: `mask_fwd`: within the 4 row blocks of one device's tokens (blocks k * 4 to k * 4 + 3), each bundle is active in at most one. `mask_bwd`: within the 4 row blocks of one device's tokens (blocks k * 4 to k * 4 + 3), each bundle is active in at most one.
All inputs are finite; a program needn't handle non-finite values.
Results may differ from the reference program's by a relative error of at most 0.0033.
Values may be sent and summed in bfloat16 or wider, within the bound.
A program may use at most 128 MiB of HBM per device.

```python
import jax
import jax.numpy as jnp
from jax import lax

D = 8192
BW = 128
BLOCK = 16
BPD = 4
TOKENS = 2048
BLOCKS = 128
BUNDLES = 32
UNITS = 4096
N_PIPE = 8
N_BUNDLE = 32


def activity_pattern(key):
    key_pos = jax.random.fold_in(key, 11)
    key_level = jax.random.fold_in(key, 12)
    key_roll = jax.random.fold_in(key, 13)
    key_force = jax.random.fold_in(key, 14)
    position = jax.random.randint(key_pos, (N_PIPE, N_BUNDLE, BUNDLES), 0, BPD)
    level = jax.random.randint(key_level, (N_PIPE, 1, BUNDLES), 1, 5)
    rolled = jax.random.randint(key_roll, (N_PIPE, N_BUNDLE, BUNDLES), 0, 4)
    forced = jax.random.randint(key_force, (N_PIPE, 1, 1), 0, BUNDLES)
    bundle_ids = jnp.arange(BUNDLES, dtype=jnp.int32)[None, None, :]
    device_ids = jnp.arange(N_BUNDLE, dtype=jnp.int32)[None, :, None]
    active = (rolled < level) | (bundle_ids == forced) & (device_ids == 0)
    block_ids = jnp.arange(BPD, dtype=jnp.int32)[None, None, :, None]
    chosen = (position[:, :, None, :] == block_ids) & active[:, :, None, :]
    return chosen.astype(jnp.int32).reshape(N_PIPE, BLOCKS, BUNDLES)


def draw_mask_fwd(key, part):
    return activity_pattern(jax.random.fold_in(key, 1))


def draw_mask_bwd(key, part):
    return activity_pattern(jax.random.fold_in(key, 2))


def level_of(stream_key, shape, pieces, low, top_value):
    factor_of, own = 1.0, jax.random.fold_in(stream_key, 6)
    for dim, parts in pieces:
        steps = jnp.exp(jax.random.uniform(jax.random.fold_in(own, dim), (parts,), jnp.float32, low / len(pieces), top_value / len(pieces)))
        factor_of = factor_of * jnp.repeat(steps, shape[dim] // parts).reshape([-1 if axis == dim else 1 for axis in range(len(shape))])
    return factor_of


def centred(stream_key, dims, scale, bound, pieces=(), held_as=jnp.bfloat16):
    level = level_of(stream_key, dims, pieces, -0.22, 0.18) if pieces else 1.0
    values = jax.random.normal(stream_key, dims, jnp.float32) * scale * level
    return jnp.minimum(jnp.maximum(values, -bound), bound).astype(held_as)


def setup_inputs(seed: int = 0) -> dict:
    key_of = jax.random.split(jax.random.key(seed), 10)
    return {
        "act_fwd": centred(key_of[0], (N_PIPE, TOKENS, D), 1.0, 6.0, ((0, 8), (1, 32))),
        "grad_in": centred(key_of[1], (N_PIPE, TOKENS, D), 1.0, 6.0, ((0, 8), (1, 32))),
        "w_gate": centred(key_of[2], (N_PIPE, D, UNITS), D ** -0.5, 0.0625, ((0, 8), (2, 32))),
        "w_up": centred(key_of[3], (N_PIPE, D, UNITS), D ** -0.5, 0.0625, ((0, 8), (2, 32))),
        "w_down": centred(key_of[4], (N_PIPE, UNITS, D), UNITS ** -0.5, 0.09375, ((0, 8), (1, 32))),
        "saved_gate": centred(key_of[5], (N_PIPE, TOKENS, UNITS), 1.0, 6.0, ((0, 8), (2, 32))),
        "saved_up": centred(key_of[6], (N_PIPE, TOKENS, UNITS), 1.0, 6.0, ((0, 8), (2, 32))),
        "mask_fwd": draw_mask_fwd(jax.random.fold_in(key_of[9], 71), 0),
        "mask_bwd": draw_mask_bwd(jax.random.fold_in(key_of[9], 71), 0),
    }


def unit_mask_of(mask_blocks):
    rows_mask = jnp.repeat(mask_blocks, BLOCK, axis=0)
    return jnp.repeat(rows_mask, BW, axis=1).astype(jnp.float32)


def forward_section(act_rows, gate_weight, up_weight, down_weight, mask_blocks):
    unit_mask = unit_mask_of(mask_blocks)
    gate_pre = jnp.dot(act_rows, gate_weight, preferred_element_type=jnp.float32)
    up_pre = jnp.dot(act_rows, up_weight, preferred_element_type=jnp.float32)
    hidden = (jnp.maximum(gate_pre, 0.0) * up_pre * unit_mask).astype(jnp.bfloat16)
    hidden_split = hidden.reshape(TOKENS, BUNDLES, BW).transpose(1, 0, 2)
    down_split = down_weight.reshape(BUNDLES, BW, D)

    def add_bundle(total, pair):
        piece = jnp.dot(pair[0], pair[1], preferred_element_type=jnp.float32).astype(jnp.bfloat16)
        piece = lax.optimization_barrier(piece)
        return total + piece.astype(jnp.float32), None

    total, unused = lax.scan(add_bundle, jnp.zeros((TOKENS, D), jnp.float32), (hidden_split, down_split))
    return (act_rows.astype(jnp.float32) + total).astype(jnp.bfloat16)


def backward_section(grad_rows, gate_weight, up_weight, down_weight, saved_gate, saved_up, mask_blocks):
    unit_mask = unit_mask_of(mask_blocks)
    grad_hidden = jnp.dot(grad_rows, down_weight.T, preferred_element_type=jnp.float32)
    gate_value = saved_gate.astype(jnp.float32)
    up_value = saved_up.astype(jnp.float32)
    grad_gate = (jnp.where(gate_value > 0, grad_hidden * up_value, 0.0) * unit_mask).astype(jnp.bfloat16)
    grad_up = (grad_hidden * jnp.maximum(gate_value, 0.0) * unit_mask).astype(jnp.bfloat16)
    gate_split = grad_gate.reshape(TOKENS, BUNDLES, BW).transpose(1, 0, 2)
    up_split = grad_up.reshape(TOKENS, BUNDLES, BW).transpose(1, 0, 2)
    wgate_split = gate_weight.reshape(D, BUNDLES, BW).transpose(1, 0, 2)
    wup_split = up_weight.reshape(D, BUNDLES, BW).transpose(1, 0, 2)

    def add_bundle(total, quad):
        piece = jnp.dot(quad[0], quad[2].T, preferred_element_type=jnp.float32)
        piece = piece + jnp.dot(quad[1], quad[3].T, preferred_element_type=jnp.float32)
        piece = lax.optimization_barrier(piece.astype(jnp.bfloat16))
        return total + piece.astype(jnp.float32), None

    total, unused = lax.scan(add_bundle, jnp.zeros((TOKENS, D), jnp.float32), (gate_split, up_split, wgate_split, wup_split))
    return (grad_rows.astype(jnp.float32) + total).astype(jnp.bfloat16)


def reference(act_fwd, grad_in, w_gate, w_up, w_down, saved_gate, saved_up, mask_fwd, mask_bwd):
    def per_section(section_args):
        act_rows, grad_rows, gate_w, up_w, down_w, gate_saved, up_saved, mask_first, mask_second = section_args
        ahead = forward_section(act_rows, gate_w, up_w, down_w, mask_first)
        behind = backward_section(grad_rows, gate_w, up_w, down_w, gate_saved, up_saved, mask_second)
        return ahead, behind

    ahead, behind = lax.map(per_section, (act_fwd, grad_in, w_gate, w_up, w_down, saved_gate, saved_up, mask_fwd, mask_bwd))
    return jnp.roll(ahead, 1, axis=0), jnp.roll(behind, -1, axis=0)
```

```python
import functools

import jax
import jax.numpy as jnp
from jax import lax
from jax.experimental import pallas as pl
from jax.experimental.pallas import tpu as pltpu
from jax.sharding import PartitionSpec as P

MESH = pl.DeviceIdType.MESH
F32, BF16 = jnp.float32, jnp.bfloat16
NZ, NY = 8, 4
BLOCK = 16
Z_REL = (0, 1, -1, 2, -2, 3, -3, 4)
RIGHT, LEFT = 0, 1
RING = 4
QUARTERS = 4


def slot_of(direction, step):
    if step == 4:
        return 7
    return 2 * step if direction == RIGHT else 2 * step - 1


def aligned(x, n):
    return pl.multiple_of(x, n)


def kernel(
    chunks,
    act_hbm,
    grad_hbm,
    wg_hbm,
    wu_hbm,
    wd_hbm,
    sg_hbm,
    su_hbm,
    mask_f,
    mask_b,
    out_f,
    out_b,
    tok_f,
    tok_b,
    wgu,
    wd,
    sg,
    su,
    hid,
    grads,
    acc,
    part,
    sbuf,
    rbuf,
    obuf,
    local_sem,
    z_send,
    z_recv,
    y_send,
    y_recv,
    s_send,
    s_recv,
    r_send,
    r_recv,
    o_send,
    o_recv,
):
    rows, width = act_hbm.shape
    half = rows // 2
    bw = wg_hbm.shape[1]
    n_pipe = lax.axis_size("pipe")
    pipe = lax.axis_index("pipe")
    k = lax.axis_index("bundle")
    z, y = k // NY, k % NY
    z_next = ((z + 1) % NZ) * NY + y
    z_prev = ((z + NZ - 1) % NZ) * NY + y
    y_next = z * NY + (y + 1) % NY
    y_prev = z * NY + (y + NY - 1) % NY
    y_far = z * NY + (y + 2) % NY
    p_next = (pipe + 1) % n_pipe
    p_prev = (pipe + n_pipe - 1) % n_pipe
    z_to = ((pipe, z_next), (pipe, z_prev))
    y_to = ((pipe, y_next), (pipe, y_prev))
    toks = (tok_f, tok_b)
    toks_hbm = (act_hbm, grad_hbm)
    cols = width // chunks
    qcols = width // QUARTERS
    per_q = chunks // QUARTERS

    def remote(src, dst, send, recv, to):
        return pltpu.make_async_remote_copy(
            src_ref=src,
            dst_ref=dst,
            send_sem=send,
            recv_sem=recv,
            device_id=to,
            device_id_type=MESH,
        )

    def token_copy(mb, d, step):
        tok = toks[mb]
        if step == 1:
            src = toks_hbm[mb]
        elif step == 4:
            src = tok.at[pl.ds(slot_of(d, 3) * rows + d * half, half), :]
        else:
            src = tok.at[pl.ds(slot_of(d, step - 1) * rows, rows), :]
        if step == 4:
            dst = tok.at[pl.ds(7 * rows + d * half, half), :]
        else:
            dst = tok.at[pl.ds(slot_of(d, step) * rows, rows), :]
        return remote(
            src, dst, z_send.at[mb, d, step - 1], z_recv.at[mb, d, step - 1], z_to[d]
        )

    hw = width // 2
    hb = bw // 2

    def weight_copy(d, piece):
        j = 2 if d == RIGHT else 1
        if piece == 0:
            src, dst = wg_hbm, wgu.at[j, :, pl.ds(0, bw)]
        elif piece == 1:
            src, dst = wu_hbm, wgu.at[j, :, pl.ds(bw, bw)]
        elif piece < 4:
            lanes = pl.ds((piece - 2) * bw, bw)
            src = wgu.at[j, pl.ds(d * hw, hw), lanes]
            dst = wgu.at[3, pl.ds(d * hw, hw), lanes]
        elif piece < 8:
            part_cols = pl.ds((piece - 4) * qcols, qcols)
            src = wd_hbm.at[:, part_cols]
            dst = wd.at[pl.ds(j * bw, bw), part_cols]
        else:
            part_cols = pl.ds((piece - 8) * qcols, qcols)
            src = wd.at[pl.ds(j * bw + d * hb, hb), part_cols]
            dst = wd.at[pl.ds(3 * bw + d * hb, hb), part_cols]
        return remote(src, dst, y_send.at[d, piece], y_recv.at[d, piece], y_to[d])

    def saved_copy(peer, which):
        to_y = (y + (1, NY - 1, 2)[peer]) % NY
        to = (pipe, (y_next, y_prev, y_far)[peer])
        j = (2, 1, 3)[peer]
        src = (sg_hbm, su_hbm)[which].at[:, to_y]
        dst = (sg, su)[which].at[j]
        return remote(src, dst, s_send.at[peer, which], s_recv.at[peer, which], to)

    def ring_copy(d, step, c):
        n = half if step == 1 else rows
        r0 = d * half if step == 1 else 0
        b = c % RING
        return remote(
            sbuf.at[d, step - 1, b, pl.ds(r0, n), :],
            rbuf.at[d, step - 1, b, pl.ds(r0, n), :],
            r_send.at[d, step - 1, b],
            r_recv.at[d, step - 1, b],
            z_to[d],
        )

    def out_copy(mb, c):
        at = pl.ds(aligned(c * cols, cols), cols)
        to = (p_next, k) if mb == 0 else (p_prev, k)
        return remote(
            obuf.at[c % RING],
            (out_f, out_b)[mb].at[:, at],
            o_send.at[c % RING],
            o_recv.at[mb, c],
            to,
        )

    local = [
        pltpu.make_async_copy(src, dst, local_sem.at[i])
        for i, (src, dst) in enumerate(
            (
                (wg_hbm, wgu.at[0, :, pl.ds(0, bw)]),
                (wu_hbm, wgu.at[0, :, pl.ds(bw, bw)]),
                (act_hbm, tok_f.at[pl.ds(0, rows), :]),
                (wd_hbm, wd.at[pl.ds(0, bw), :]),
                (grad_hbm, tok_b.at[pl.ds(0, rows), :]),
                (sg_hbm.at[:, y], sg.at[0]),
                (su_hbm.at[:, y], su.at[0]),
            )
        )
    ]

    barrier = pltpu.get_barrier_semaphore()
    for to in z_to + y_to + ((pipe, y_far), (p_next, k), (p_prev, k)):
        pl.semaphore_signal(barrier, inc=1, device_id=to, device_id_type=MESH)
    pl.semaphore_wait(barrier, 7)

    for mb in (0, 1):
        for d in (0, 1):
            token_copy(mb, d, 1).start()
    for piece in (0, 1):
        for d in (0, 1):
            weight_copy(d, piece).start()
    for copy in local:
        copy.start()

    def pass_tokens(mb, step):
        for d in (0, 1):
            token_copy(mb, d, step).wait_recv()
            if step < 4:
                token_copy(mb, d, step + 1).start()

    def pass_weights(piece, onward):
        for d in (0, 1):
            weight_copy(d, piece).wait_recv()
            weight_copy(d, onward).start()

    deep = width // 8

    def hidden_for(j_from, j_to, first_slot, slots):
        r0, m = first_slot * rows, slots * rows

        @pl.loop(j_from, j_to)
        def _(j):
            both = pl.ds(0, 2 * bw)
            acc[pl.ds(0, m), both] = jnp.zeros((m, 2 * bw), F32)

            @pl.loop(0, 8)
            def _(kc):
                at = pl.ds(aligned(kc * deep, deep), deep)
                acc[pl.ds(0, m), both] += jnp.dot(
                    tok_f[pl.ds(r0, m), at], wgu[j, at, :], preferred_element_type=F32
                )

            bundle = z * NY + (y + j + j // 2 - 2 * (j // 3)) % NY
            lanes = pl.ds(aligned(j * bw, bw), bw)
            for i in range(slots):
                owner = (z + NZ + Z_REL[first_slot + i]) % NZ
                for b in range(rows // BLOCK):
                    block = (owner * NY + y) * (rows // BLOCK) + b
                    on = mask_f[block, bundle].astype(F32)
                    a0 = i * rows + b * BLOCK
                    gate = acc[pl.ds(a0, BLOCK), pl.ds(0, bw)]
                    up = acc[pl.ds(a0, BLOCK), pl.ds(bw, bw)]
                    hid[pl.ds(r0 + a0, BLOCK), lanes] = (
                        jnp.maximum(gate, 0.0) * up * on
                    ).astype(BF16)

    pass_tokens(0, 1)
    pass_tokens(1, 1)
    pass_weights(0, 2)
    pass_tokens(0, 2)
    pass_tokens(1, 2)
    pass_weights(1, 3)
    for d in (0, 1):
        weight_copy(d, 4).start()
    pass_tokens(0, 3)
    for copy in local:
        copy.wait()
    hidden_for(0, 3, 0, 7)
    pass_tokens(1, 3)
    for d in (0, 1):
        weight_copy(d, 2).wait_recv()
        weight_copy(d, 3).wait_recv()
    hidden_for(3, 4, 0, 7)
    pass_tokens(0, 4)
    hidden_for(0, 4, 7, 1)
    pass_weights(4, 8)
    for d in (0, 1):
        weight_copy(d, 5).start()

    gh = acc
    n_part = part.shape[0]

    def grads_for():
        for j in range(NY):
            rel = (0, 1, 3, 2)[j]
            bundle = z * NY + (y + rel) % NY
            for i in range(NZ):
                owner = (z + NZ + Z_REL[i]) % NZ
                for b in range(rows // BLOCK):
                    block = (owner * NY + y) * (rows // BLOCK) + b
                    on = mask_b[block, bundle].astype(F32)
                    at = pl.ds(i * rows + b * BLOCK, BLOCK)
                    grad = gh[at, pl.ds(j * bw, bw)] * on
                    in_block = pl.ds(b * BLOCK, BLOCK)
                    gate = sg[j, owner, in_block, :].astype(F32)
                    up = su[j, owner, in_block, :].astype(F32)
                    grads[at, pl.ds(2 * j * bw, bw)] = jnp.where(
                        gate > 0, grad * up, 0.0
                    ).astype(BF16)
                    grads[at, pl.ds((2 * j + 1) * bw, bw)] = (
                        grad * jnp.maximum(gate, 0.0)
                    ).astype(BF16)

    def side_work(t):
        for q in range(1, QUARTERS):

            @pl.when(t == 3 * q - 2)
            def _():
                pass_weights(4 + q, 8 + q)
                if q < QUARTERS - 1:
                    for d in (0, 1):
                        weight_copy(d, 5 + q).start()
                else:
                    for peer in range(3):
                        for which in (0, 1):
                            saved_copy(peer, which).start()

        for q in range(QUARTERS):

            @pl.when(t == per_q * q)
            def _():
                for d in (0, 1):
                    weight_copy(d, 8 + q).wait_recv()

        @pl.when(t == chunks - 8)
        def _():
            for d in (0, 1):
                token_copy(1, d, 4).wait_recv()
            gh[:, :] = jnp.zeros(gh.shape, F32)

        @pl.when((t >= chunks - 8) & (t < chunks))
        def _():
            at = pl.ds(aligned((t - (chunks - 8)) * deep, deep), deep)
            gh[:, :] += lax.dot_general(
                tok_b[:, at],
                wd[:, at],
                (((1,), (1,)), ((), ())),
                preferred_element_type=F32,
            )

        @pl.when(t == chunks - 1)
        def _():
            for peer in range(3):
                for which in (0, 1):
                    saved_copy(peer, which).wait_recv()
            grads_for()

    def local_part(t):
        @pl.when(t < chunks)
        def _():
            at = pl.ds(aligned(t * cols, cols), cols)
            part[t % n_part] = jnp.dot(hid[...], wd[:, at], preferred_element_type=F32)

        @pl.when((t >= chunks) & (t < 2 * chunks))
        def _():
            at = pl.ds(aligned((t - chunks) * cols, cols), cols)
            total = None
            for j in range(NY):
                piece = lax.dot_general(
                    grads[:, pl.ds(2 * j * bw, 2 * bw)],
                    wgu[j, at, :],
                    (((1,), (1,)), ((), ())),
                    preferred_element_type=F32,
                )
                total = piece if total is None else total + piece
            part[t % n_part] = total

    def ring_step(step, c):
        b = c % RING
        pb = c % n_part
        for d in (0, 1):
            if step > 1:
                ring_copy(d, step - 1, c).wait_recv()

            @pl.when(c >= RING)
            def _():
                ring_copy(d, step, c - RING).wait_send()

            slot = 7 if step == 1 else slot_of(1 - d, 5 - step)
            lo, hi = pl.ds(0, half), pl.ds(half, half)
            mine = pl.ds(d * half, half)
            other = pl.ds((1 - d) * half, half)
            if step == 1:
                at = pl.ds(slot * rows + d * half, half)
                sbuf[d, 0, b, mine, :] = part[pb, at, :].astype(BF16)
            elif step == 2:
                at = pl.ds(slot * rows + d * half, half)
                to = pl.ds(slot * rows + (1 - d) * half, half)
                sbuf[d, 1, b, mine, :] = (
                    part[pb, at, :] + rbuf[d, 0, b, mine, :].astype(F32)
                ).astype(BF16)
                sbuf[d, 1, b, other, :] = part[pb, to, :].astype(BF16)
            else:
                at = pl.ds(slot * rows, rows)
                sbuf[d, step - 1, b] = (
                    part[pb, at, :] + rbuf[d, step - 2, b].astype(F32)
                ).astype(BF16)
            ring_copy(d, step, c).start()

    def finish(c):
        b = c % RING
        for d in (0, 1):
            ring_copy(d, 4, c).wait_recv()

        @pl.when(c >= RING)
        def _():
            out_copy(0, 0 * c + (c - RING) % chunks).wait_send()

        arrived = (
            part[c % n_part, pl.ds(0, rows), :]
            + rbuf[0, 3, b].astype(F32)
            + rbuf[1, 3, b].astype(F32)
        )
        for mb in (0, 1):

            @pl.when((c >= mb * chunks) & (c < (mb + 1) * chunks))
            def _():
                cc = c - mb * chunks
                at = pl.ds(aligned(cc * cols, cols), cols)
                base = toks[mb][pl.ds(0, rows), at].astype(F32)
                obuf[b] = (base + arrived).astype(BF16)
                out_copy(mb, cc).start()

    total = 2 * chunks

    @pl.loop(0, total + 4)
    def _(t):
        side_work(t)
        local_part(t)
        for step in range(1, 5):

            @pl.when((t >= step - 1) & (t < total + step - 1))
            def _():
                ring_step(step, t - (step - 1))

        @pl.when(t >= 4)
        def _():
            finish(t - 4)

    @pl.loop(total - RING, total)
    def _(c):
        for d in (0, 1):
            for step in range(1, 5):
                ring_copy(d, step, c).wait_send()
        out_copy(1, c - chunks).wait_send()

    for mb in (0, 1):
        for d in (0, 1):
            for step in range(1, 5):
                token_copy(mb, d, step).wait_send()
    for d in (0, 1):
        for piece in range(12):
            weight_copy(d, piece).wait_send()
    for peer in range(3):
        for which in (0, 1):
            saved_copy(peer, which).wait_send()

    @pl.loop(0, chunks)
    def _(c):
        for mb in (0, 1):
            out_copy(mb, c).wait_recv()


def per_device(act_fwd, grad_in, w_gate, w_up, w_down, saved_gate, saved_up, mask_fwd, mask_bwd):
    rows, width = act_fwd.shape[1:]
    bw = w_gate.shape[2]
    chunks = 16
    cols = width // chunks
    all_rows = NZ * rows
    by_owner = (NZ, NY, rows, bw)
    anywhere = pl.BlockSpec(memory_space=pl.ANY)
    scalars = pl.BlockSpec(memory_space=pltpu.SMEM)
    dma = pltpu.SemaphoreType.DMA
    out = jax.ShapeDtypeStruct((rows, width), BF16)
    ahead, behind = pl.pallas_call(
        functools.partial(kernel, chunks),
        out_shape=(out, out),
        in_specs=[anywhere] * 7 + [scalars] * 2,
        out_specs=(anywhere, anywhere),
        scratch_shapes=[
            pltpu.VMEM((all_rows, width), BF16),
            pltpu.VMEM((all_rows, width), BF16),
            pltpu.VMEM((NY, width, 2 * bw), BF16),
            pltpu.VMEM((NY * bw, width), BF16),
            pltpu.VMEM((NY, NZ, rows, bw), BF16),
            pltpu.VMEM((NY, NZ, rows, bw), BF16),
            pltpu.VMEM((all_rows, NY * bw), BF16),
            pltpu.VMEM((all_rows, 2 * NY * bw), BF16),
            pltpu.VMEM((all_rows, NY * bw), F32),
            pltpu.VMEM((5, all_rows, cols), F32),
            pltpu.VMEM((2, 4, RING, rows, cols), BF16),
            pltpu.VMEM((2, 4, RING, rows, cols), BF16),
            pltpu.VMEM((RING, rows, cols), BF16),
            dma((7,)),
            dma((2, 2, 4)),
            dma((2, 2, 4)),
            dma((2, 12)),
            dma((2, 12)),
            dma((3, 2)),
            dma((3, 2)),
            dma((2, 4, RING)),
            dma((2, 4, RING)),
            dma((RING,)),
            dma((2, chunks)),
        ],
        compiler_params=pltpu.CompilerParams(
            collective_id=0, has_side_effects=True, vmem_limit_bytes=67043328
        ),
    )(
        act_fwd[0],
        grad_in[0],
        w_gate[0],
        w_up[0],
        w_down[0],
        saved_gate[0].reshape(by_owner),
        saved_up[0].reshape(by_owner),
        mask_fwd[0],
        mask_bwd[0],
    )
    return ahead[None], behind[None]


def solution(mesh):
    in_specs = (
        P("pipe", "bundle", None),
        P("pipe", "bundle", None),
        P("pipe", None, "bundle"),
        P("pipe", None, "bundle"),
        P("pipe", "bundle", None),
        P("pipe", None, "bundle"),
        P("pipe", None, "bundle"),
        P("pipe", None, None),
        P("pipe", None, None),
    )
    out_specs = (P("pipe", "bundle", None), P("pipe", "bundle", None))
    return jax.shard_map(
        per_device, mesh=mesh, in_specs=in_specs, out_specs=out_specs, check_vma=False
    )
```

```python
import functools

import jax
import jax.numpy as jnp
from jax import lax
from jax.experimental import pallas as pl
from jax.experimental.pallas import tpu as pltpu
from jax.sharding import PartitionSpec as P

MESH = pl.DeviceIdType.MESH
F32, BF16 = jnp.float32, jnp.bfloat16
NZ, NY = 8, 4
BLOCK = 16
Z_REL = (0, 1, -1, 2, -2, 3, -3, 4)
RIGHT, LEFT = 0, 1
RING = 8
LAG = 4
QUARTERS = 4


def slot_of(direction, step):
    if step == 4:
        return 7
    return 2 * step if direction == RIGHT else 2 * step - 1


def aligned(x, n):
    return pl.multiple_of(x, n)


def kernel(
    chunks,
    act_hbm,
    grad_hbm,
    wg_hbm,
    wu_hbm,
    wd_hbm,
    sg_hbm,
    su_hbm,
    mask_f,
    mask_b,
    out_f,
    out_b,
    tok_f,
    tok_b,
    wgu,
    wd,
    sg,
    su,
    hid,
    grads,
    acc,
    part,
    sbuf,
    rbuf,
    obuf,
    local_sem,
    z_send,
    z_recv,
    y_send,
    y_recv,
    s_send,
    s_recv,
    r_send,
    r_recv,
    o_send,
    o_recv,
):
    rows, width = act_hbm.shape
    half = rows // 2
    bw = wg_hbm.shape[1]
    n_pipe = lax.axis_size("pipe")
    pipe = lax.axis_index("pipe")
    k = lax.axis_index("bundle")
    z, y = k // NY, k % NY
    z_next = ((z + 1) % NZ) * NY + y
    z_prev = ((z + NZ - 1) % NZ) * NY + y
    y_next = z * NY + (y + 1) % NY
    y_prev = z * NY + (y + NY - 1) % NY
    y_far = z * NY + (y + 2) % NY
    p_next = (pipe + 1) % n_pipe
    p_prev = (pipe + n_pipe - 1) % n_pipe
    z_to = ((pipe, z_next), (pipe, z_prev))
    y_to = ((pipe, y_next), (pipe, y_prev))
    toks = (tok_f, tok_b)
    toks_hbm = (act_hbm, grad_hbm)
    cols = width // chunks
    qcols = width // QUARTERS
    per_q = chunks // QUARTERS

    def remote(src, dst, send, recv, to):
        return pltpu.make_async_remote_copy(
            src_ref=src,
            dst_ref=dst,
            send_sem=send,
            recv_sem=recv,
            device_id=to,
            device_id_type=MESH,
        )

    def token_copy(mb, d, step, h):
        tok = toks[mb]
        if step == 1:
            src = toks_hbm[mb].at[pl.ds(h * half, half), :]
        else:
            src = tok.at[pl.ds(slot_of(d, step - 1) * rows + h * half, half), :]
        dst = tok.at[pl.ds(slot_of(d, step) * rows + h * half, half), :]
        at = (mb, d, step - 1, h)
        return remote(src, dst, z_send.at[at], z_recv.at[at], z_to[d])

    hw = width // 2
    hb = bw // 2

    def weight_copy(d, piece):
        j = 2 if d == RIGHT else 1
        if piece == 0:
            src, dst = wg_hbm, wgu.at[j, :, pl.ds(0, bw)]
        elif piece == 1:
            src, dst = wu_hbm, wgu.at[j, :, pl.ds(bw, bw)]
        elif piece < 4:
            lanes = pl.ds((piece - 2) * bw, bw)
            src = wgu.at[j, pl.ds(d * hw, hw), lanes]
            dst = wgu.at[3, pl.ds(d * hw, hw), lanes]
        elif piece < 8:
            part_cols = pl.ds((piece - 4) * qcols, qcols)
            src = wd_hbm.at[:, part_cols]
            dst = wd.at[pl.ds(j * bw, bw), part_cols]
        else:
            part_cols = pl.ds((piece - 8) * qcols, qcols)
            src = wd.at[pl.ds(j * bw + d * hb, hb), part_cols]
            dst = wd.at[pl.ds(3 * bw + d * hb, hb), part_cols]
        return remote(src, dst, y_send.at[d, piece], y_recv.at[d, piece], y_to[d])

    def saved_copy(peer, which):
        to_y = (y + (1, NY - 1, 2)[peer]) % NY
        to = (pipe, (y_next, y_prev, y_far)[peer])
        j = (2, 1, 3)[peer]
        src = (sg_hbm, su_hbm)[which].at[:, to_y]
        dst = (sg, su)[which].at[j]
        return remote(src, dst, s_send.at[peer, which], s_recv.at[peer, which], to)

    def ring_copy(d, step, c):
        n = half if step == 1 else rows
        r0 = d * half if step == 1 else 0
        b = c % RING
        return remote(
            sbuf.at[d, step - 1, b, pl.ds(r0, n), :],
            rbuf.at[d, step - 1, b, pl.ds(r0, n), :],
            r_send.at[d, step - 1, b],
            r_recv.at[d, step - 1, b],
            z_to[d],
        )

    def out_copy(mb, c):
        at = pl.ds(aligned(c * cols, cols), cols)
        to = (p_next, k) if mb == 0 else (p_prev, k)
        return remote(
            obuf.at[c % RING],
            (out_f, out_b)[mb].at[:, at],
            o_send.at[c % RING],
            o_recv.at[mb, c],
            to,
        )

    local = [
        pltpu.make_async_copy(src, dst, local_sem.at[i])
        for i, (src, dst) in enumerate(
            (
                (wg_hbm, wgu.at[0, :, pl.ds(0, bw)]),
                (wu_hbm, wgu.at[0, :, pl.ds(bw, bw)]),
                (act_hbm, tok_f.at[pl.ds(0, rows), :]),
                (wd_hbm, wd.at[pl.ds(0, bw), :]),
                (grad_hbm, tok_b.at[pl.ds(0, rows), :]),
                (sg_hbm.at[:, y], sg.at[0]),
                (su_hbm.at[:, y], su.at[0]),
            )
        )
    ]

    barrier = pltpu.get_barrier_semaphore()
    for to in z_to + y_to + ((pipe, y_far), (p_next, k), (p_prev, k)):
        pl.semaphore_signal(barrier, inc=1, device_id=to, device_id_type=MESH)
    pl.semaphore_wait(barrier, 7)

    def send_tokens(mb):
        for h in (0, 1):
            for d in (0, 1):
                token_copy(mb, d, 1, h).start()

    send_tokens(0)
    for piece in (0, 1):
        for d in (0, 1):
            weight_copy(d, piece).start()
    for copy in local:
        copy.start()

    def pass_tokens(mb, step, h):
        for d in (0, 1):
            token_copy(mb, d, step, h).wait_recv()
            if step < 3 or h == d:
                token_copy(mb, d, step + 1, h).start()

    def last_tokens(mb):
        for d in (0, 1):
            token_copy(mb, d, 4, d).wait_recv()

    def pass_weights(piece, onward):
        for d in (0, 1):
            weight_copy(d, piece).wait_recv()
            weight_copy(d, onward).start()

    deep = width // 8

    def hidden_for(j_from, j_to):
        @pl.loop(j_from, j_to)
        def _(j):
            both = pl.ds(0, 2 * bw)
            acc[:, both] = jnp.zeros((NZ * rows, 2 * bw), F32)

            @pl.loop(0, 8)
            def _(kc):
                at = pl.ds(aligned(kc * deep, deep), deep)
                acc[:, both] += jnp.dot(
                    tok_f[:, at], wgu[j, at, :], preferred_element_type=F32
                )

            bundle = z * NY + (y + j + j // 2 - 2 * (j // 3)) % NY
            lanes = pl.ds(aligned(j * bw, bw), bw)
            for i in range(NZ):
                owner = (z + NZ + Z_REL[i]) % NZ
                for b in range(rows // BLOCK):
                    block = (owner * NY + y) * (rows // BLOCK) + b
                    on = mask_f[bundle, block].astype(F32)
                    a0 = i * rows + b * BLOCK
                    gate = acc[pl.ds(a0, BLOCK), pl.ds(0, bw)]
                    up = acc[pl.ds(a0, BLOCK), pl.ds(bw, bw)]
                    hid[pl.ds(a0, BLOCK), lanes] = (
                        jnp.maximum(gate, 0.0) * up * on
                    ).astype(BF16)

    for step in (1, 2):
        for h in (0, 1):
            pass_tokens(0, step, h)
    pass_weights(0, 2)
    for h in (0, 1):
        pass_tokens(0, 3, h)
    send_tokens(1)
    last_tokens(0)
    pass_weights(1, 3)
    for d in (0, 1):
        weight_copy(d, 4).start()
    for h in (0, 1):
        pass_tokens(1, 1, h)
    for copy in local:
        copy.wait()
    hidden_for(0, 3)
    for h in (0, 1):
        pass_tokens(1, 2, h)
    for d in (0, 1):
        weight_copy(d, 2).wait_recv()
        weight_copy(d, 3).wait_recv()
    hidden_for(3, 4)
    for h in (0, 1):
        pass_tokens(1, 3, h)
    pass_weights(4, 8)
    for d in (0, 1):
        weight_copy(d, 5).start()

    gh = acc
    n_part = part.shape[0]

    def grads_for():
        for j in range(NY):
            rel = (0, 1, 3, 2)[j]
            bundle = z * NY + (y + rel) % NY
            for i in range(NZ):
                owner = (z + NZ + Z_REL[i]) % NZ
                for b in range(rows // BLOCK):
                    block = (owner * NY + y) * (rows // BLOCK) + b
                    on = mask_b[bundle, block].astype(F32)
                    at = pl.ds(i * rows + b * BLOCK, BLOCK)
                    grad = gh[at, pl.ds(j * bw, bw)] * on
                    in_block = pl.ds(b * BLOCK, BLOCK)
                    gate = sg[j, owner, in_block, :].astype(F32)
                    up = su[j, owner, in_block, :].astype(F32)
                    grads[at, pl.ds(2 * j * bw, bw)] = jnp.where(
                        gate > 0, grad * up, 0.0
                    ).astype(BF16)
                    grads[at, pl.ds((2 * j + 1) * bw, bw)] = (
                        grad * jnp.maximum(gate, 0.0)
                    ).astype(BF16)

    def side_work(t):
        for q in range(1, QUARTERS):

            @pl.when(t == 4 * q - 2)
            def _():
                pass_weights(4 + q, 8 + q)
                if q < QUARTERS - 1:
                    for d in (0, 1):
                        weight_copy(d, 5 + q).start()
                else:
                    for peer in range(3):
                        for which in (0, 1):
                            saved_copy(peer, which).start()

        for q in range(QUARTERS):

            @pl.when(t == per_q * q)
            def _():
                for d in (0, 1):
                    weight_copy(d, 8 + q).wait_recv()

        @pl.when(t == chunks - 8)
        def _():
            last_tokens(1)
            gh[:, :] = jnp.zeros(gh.shape, F32)

        @pl.when((t >= chunks - 8) & (t < chunks))
        def _():
            at = pl.ds(aligned((t - (chunks - 8)) * deep, deep), deep)
            gh[:, :] += lax.dot_general(
                tok_b[:, at],
                wd[:, at],
                (((1,), (1,)), ((), ())),
                preferred_element_type=F32,
            )

        @pl.when(t == chunks - 1)
        def _():
            for peer in range(3):
                for which in (0, 1):
                    saved_copy(peer, which).wait_recv()
            grads_for()

    def local_part(t):
        @pl.when(t < chunks)
        def _():
            at = pl.ds(aligned(t * cols, cols), cols)
            part[t % n_part] = jnp.dot(hid[...], wd[:, at], preferred_element_type=F32)

        @pl.when((t >= chunks) & (t < 2 * chunks))
        def _():
            at = pl.ds(aligned((t - chunks) * cols, cols), cols)
            total = None
            for j in range(NY):
                piece = lax.dot_general(
                    grads[:, pl.ds(2 * j * bw, 2 * bw)],
                    wgu[j, at, :],
                    (((1,), (1,)), ((), ())),
                    preferred_element_type=F32,
                )
                total = piece if total is None else total + piece
            part[t % n_part] = total

    def ring_step(step, c):
        b = c % RING
        pb = c % n_part
        for d in (0, 1):
            if step > 1:
                ring_copy(d, step - 1, c).wait_recv()

            @pl.when(c >= RING)
            def _():
                ring_copy(d, step, c - RING).wait_send()

            slot = 7 if step == 1 else slot_of(1 - d, 5 - step)
            lo, hi = pl.ds(0, half), pl.ds(half, half)
            mine = pl.ds(d * half, half)
            other = pl.ds((1 - d) * half, half)
            if step == 1:
                at = pl.ds(slot * rows + d * half, half)
                sbuf[d, 0, b, mine, :] = part[pb, at, :].astype(BF16)
            elif step == 2:
                at = pl.ds(slot * rows + d * half, half)
                to = pl.ds(slot * rows + (1 - d) * half, half)
                sbuf[d, 1, b, mine, :] = (
                    part[pb, at, :] + rbuf[d, 0, b, mine, :].astype(F32)
                ).astype(BF16)
                sbuf[d, 1, b, other, :] = part[pb, to, :].astype(BF16)
            else:
                at = pl.ds(slot * rows, rows)
                sbuf[d, step - 1, b] = (
                    part[pb, at, :] + rbuf[d, step - 2, b].astype(F32)
                ).astype(BF16)
            ring_copy(d, step, c).start()

    def finish(c):
        b = c % RING
        for d in (0, 1):
            ring_copy(d, 4, c).wait_recv()

        @pl.when(c >= RING)
        def _():
            out_copy(0, (c - RING) % chunks).wait_send()

        arrived = (
            part[c % n_part, pl.ds(0, rows), :]
            + rbuf[0, 3, b].astype(F32)
            + rbuf[1, 3, b].astype(F32)
        )
        for mb in (0, 1):

            @pl.when((c >= mb * chunks) & (c < (mb + 1) * chunks))
            def _():
                cc = c - mb * chunks
                at = pl.ds(aligned(cc * cols, cols), cols)
                base = toks[mb][pl.ds(0, rows), at].astype(F32)
                obuf[b] = (base + arrived).astype(BF16)
                out_copy(mb, cc).start()

    total = 2 * chunks

    behind = (0, 1, 2, 3 + LAG, 4 + LAG)

    @pl.loop(0, total + behind[4])
    def _(t):
        side_work(t)
        local_part(t)
        for step in range(1, 5):
            late = behind[step - 1]

            @pl.when((t >= late) & (t < total + late))
            def _():
                ring_step(step, t - late)

        @pl.when(t >= behind[4])
        def _():
            finish(t - behind[4])

    @pl.loop(total - RING, total)
    def _(c):
        for d in (0, 1):
            for step in range(1, 5):
                ring_copy(d, step, c).wait_send()
        out_copy(1, c - chunks).wait_send()

    for mb in (0, 1):
        for d in (0, 1):
            for step in (1, 2, 3):
                for h in (0, 1):
                    token_copy(mb, d, step, h).wait_send()
            token_copy(mb, d, 4, d).wait_send()
    for d in (0, 1):
        for piece in range(12):
            weight_copy(d, piece).wait_send()
    for peer in range(3):
        for which in (0, 1):
            saved_copy(peer, which).wait_send()

    @pl.loop(0, chunks)
    def _(c):
        for mb in (0, 1):
            out_copy(mb, c).wait_recv()


def per_device(act_fwd, grad_in, w_gate, w_up, w_down, saved_gate, saved_up, mask_fwd, mask_bwd):
    rows, width = act_fwd.shape[1:]
    bw = w_gate.shape[2]
    chunks = 16
    cols = width // chunks
    all_rows = NZ * rows
    by_owner = (NZ, NY, rows, bw)
    anywhere = pl.BlockSpec(memory_space=pl.ANY)
    scalars = pl.BlockSpec(memory_space=pltpu.SMEM)
    dma = pltpu.SemaphoreType.DMA
    out = jax.ShapeDtypeStruct((rows, width), BF16)
    ahead, behind = pl.pallas_call(
        functools.partial(kernel, chunks),
        out_shape=(out, out),
        in_specs=[anywhere] * 7 + [scalars] * 2,
        out_specs=(anywhere, anywhere),
        scratch_shapes=[
            pltpu.VMEM((all_rows, width), BF16),
            pltpu.VMEM((all_rows, width), BF16),
            pltpu.VMEM((NY, width, 2 * bw), BF16),
            pltpu.VMEM((NY * bw, width), BF16),
            pltpu.VMEM((NY, NZ, rows, bw), BF16),
            pltpu.VMEM((NY, NZ, rows, bw), BF16),
            pltpu.VMEM((all_rows, NY * bw), BF16),
            pltpu.VMEM((all_rows, 2 * NY * bw), BF16),
            pltpu.VMEM((all_rows, NY * bw), F32),
            pltpu.VMEM((5 + LAG, all_rows, cols), F32),
            pltpu.VMEM((2, 4, RING, rows, cols), BF16),
            pltpu.VMEM((2, 4, RING, rows, cols), BF16),
            pltpu.VMEM((RING, rows, cols), BF16),
            dma((7,)),
            dma((2, 2, 4, 2)),
            dma((2, 2, 4, 2)),
            dma((2, 12)),
            dma((2, 12)),
            dma((3, 2)),
            dma((3, 2)),
            dma((2, 4, RING)),
            dma((2, 4, RING)),
            dma((RING,)),
            dma((2, chunks)),
        ],
        compiler_params=pltpu.CompilerParams(
            collective_id=0, has_side_effects=True, vmem_limit_bytes=67043328
        ),
    )(
        act_fwd[0],
        grad_in[0],
        w_gate[0],
        w_up[0],
        w_down[0],
        saved_gate[0].reshape(by_owner),
        saved_up[0].reshape(by_owner),
        mask_fwd[0].T,
        mask_bwd[0].T,
    )
    return ahead[None], behind[None]


def solution(mesh):
    in_specs = (
        P("pipe", "bundle", None),
        P("pipe", "bundle", None),
        P("pipe", None, "bundle"),
        P("pipe", None, "bundle"),
        P("pipe", "bundle", None),
        P("pipe", None, "bundle"),
        P("pipe", None, "bundle"),
        P("pipe", None, None),
        P("pipe", None, None),
    )
    out_specs = (P("pipe", "bundle", None), P("pipe", "bundle", None))
    return jax.shard_map(
        per_device, mesh=mesh, in_specs=in_specs, out_specs=out_specs, check_vma=False
    )
```

```python
import functools

import jax
import jax.numpy as jnp
from jax import lax
from jax.experimental import pallas as pl
from jax.experimental.pallas import tpu as pltpu
from jax.sharding import PartitionSpec as P

MESH = pl.DeviceIdType.MESH
F32, BF16 = jnp.float32, jnp.bfloat16
NZ, NY = 8, 4
BLOCK = 16
Z_REL = (0, 1, -1, 2, -2, 3, -3, 4)
RIGHT, LEFT = 0, 1
RING = 4
QUARTERS = 4
STEPS = 5
FOREIGN = (-1, -2, 1, 2)
FOREIGN_PLACE = (0, 0, 3, 3)


def slot_at(rel):
    rel = (rel + 3) % NZ - 3
    return Z_REL.index(rel)


def aligned(x, n):
    return pl.multiple_of(x, n)


def dot_last(a, b):
    return lax.dot_general(a, b, (((1,), (1,)), ((), ())), preferred_element_type=F32)


def kernel(chunks, *refs):
    (act_hbm, grad_hbm, wg_hbm, wu_hbm, wd_hbm, sg_hbm, su_hbm, mask_f, mask_b) = refs[:9]
    out_f, out_b = refs[9:11]
    (tok_f, tok_b, wgu, wd, sg, su, hid, acc, base_f) = refs[11:20]
    (pk_own, pk_send, pk_recv, hidp, hid_recv) = refs[20:25]
    (ghp, gh_send, gh_recv, gradp, grad_recv) = refs[25:30]
    part, obuf = refs[30:32]
    sbufs, rbufs = refs[32:37], refs[37:42]
    (local_sem, z_send, z_recv, w_send, w_recv, y_send, y_recv, s_send, s_recv) = refs[42:51]
    (x_send, x_recv, r_send, r_recv, o_send, o_recv) = refs[51:57]

    rows, width = act_hbm.shape
    bw = wg_hbm.shape[1]
    pw = width // NZ
    blocks = rows // BLOCK
    n_pipe = lax.axis_size("pipe")
    pipe = lax.axis_index("pipe")
    k = lax.axis_index("bundle")
    z, y = k // NY, k % NY

    def at_z(step):
        return (pipe, ((z + NZ + step) % NZ) * NY + y)

    def at_y(step):
        return (pipe, z * NY + (y + NY + step) % NY)

    p_next = (pipe + 1) % n_pipe
    p_prev = (pipe + n_pipe - 1) % n_pipe
    z_to = (at_z(1), at_z(-1))
    y_to = (at_y(1), at_y(-1))
    toks = (tok_f, tok_b)
    cols = pw // chunks
    qcols = pw // QUARTERS

    def remote(src, dst, send, recv, to):
        return pltpu.make_async_remote_copy(
            src_ref=src,
            dst_ref=dst,
            send_sem=send,
            recv_sem=recv,
            device_id=to,
            device_id_type=MESH,
        )

    def part_of(place):
        return (z + 2 * NZ - place) % NZ

    def part_at(e):
        return pl.ds(aligned(e * pw, pw), pw)

    def token_copy(mb, d, step):
        tok = toks[mb]
        n = (STEPS + 1 - step) * pw
        sign = -1 if d == RIGHT else 1
        first, then = ((step - 1) * pw, step * pw) if d == RIGHT else (3 * pw, 2 * pw)
        src = tok.at[pl.ds(slot_at(sign * (step - 1)) * rows, rows), pl.ds(first, n)]
        dst = tok.at[pl.ds(slot_at(sign * step) * rows, rows), pl.ds(then, n)]
        at = (mb, d, step - 1)
        return remote(src, dst, z_send.at[at], z_recv.at[at], z_to[d])

    def shared_weight(f, which):
        e = (z + NZ + (1, 2, -4, -5)[f]) % NZ
        to = at_z((1, 2, -1, -2)[f])
        if which < 2:
            src = (wg_hbm, wu_hbm)[which].at[part_at(e), :]
            dst = wgu.at[pl.ds((4 + f) * pw, pw), pl.ds(which * bw, bw)]
        else:
            src = wd_hbm.at[:, part_at(e)]
            dst = wd.at[4 + f, pl.ds(0, bw), :]
        return remote(src, dst, w_send.at[f, which], w_recv.at[f, which], to)

    def weight_copy(d, piece):
        j = 2 if d == RIGHT else 1
        half = 2 * pw
        if piece < 2:
            at = pl.ds(piece * 4 * pw, 4 * pw)
            src = wgu.at[at, pl.ds(0, 2 * bw)]
            dst = wgu.at[at, pl.ds(j * 2 * bw, 2 * bw)]
        elif piece < 4:
            at = pl.ds((piece - 2) * 4 * pw + d * half, half)
            src = wgu.at[at, pl.ds(j * 2 * bw, 2 * bw)]
            dst = wgu.at[at, pl.ds(3 * 2 * bw, 2 * bw)]
        elif piece < 8:
            at = pl.ds((piece - 4) * qcols, qcols)
            src = wd.at[:, pl.ds(0, bw), at]
            dst = wd.at[:, pl.ds(j * bw, bw), at]
        else:
            at = pl.ds((piece - 8) * qcols, qcols)
            hb = bw // 2
            src = wd.at[:, pl.ds(j * bw + d * hb, hb), at]
            dst = wd.at[:, pl.ds(3 * bw + d * hb, hb), at]
        return remote(src, dst, y_send.at[d, piece], y_recv.at[d, piece], y_to[d])

    def saved_copy(peer, which):
        step = (1, -1, 2)[peer]
        src = (sg_hbm, su_hbm)[which].at[:, (y + NY + step) % NY]
        dst = (sg, su)[which].at[(2, 1, 3)[peer]]
        at = (peer, which)
        return remote(src, dst, s_send.at[at], s_recv.at[at], at_y(step))

    def to_owner(src, dst, kind, f):
        return remote(
            src.at[f], dst.at[f], x_send.at[kind, f], x_recv.at[kind, f], at_z(FOREIGN[f])
        )

    def to_helper(src, dst, kind, f):
        return remote(
            src, dst.at[f], x_send.at[kind, f], x_recv.at[kind, f], at_z(-FOREIGN[f])
        )

    def ring_copy(d, step, c):
        b = c % RING
        return remote(
            sbufs[step - 1].at[d, b],
            rbufs[step - 1].at[d, b],
            r_send.at[d, step - 1, b],
            r_recv.at[d, step - 1, b],
            z_to[d],
        )

    def out_copy(mb, c, i):
        e = part_of(i - 2)
        to = (p_next, k) if mb == 0 else (p_prev, k)
        return remote(
            obuf.at[c % RING, :, pl.ds(i * cols, cols)],
            (out_f, out_b)[mb].at[:, pl.ds(aligned(e * pw + c * cols, cols), cols)],
            o_send.at[c % RING, i],
            o_recv.at[mb, c, i],
            to,
        )

    own_rows = pl.ds(0, rows)
    pairs = []
    for i in range(NZ):
        pairs.append(
            (act_hbm.at[:, part_at(part_of(i - 2))], tok_f.at[own_rows, pl.ds(i * pw, pw)])
        )
    for p in range(4):
        e = part_at(part_of(p))
        pairs.append((wg_hbm.at[e, :], wgu.at[pl.ds(p * pw, pw), pl.ds(0, bw)]))
        pairs.append((wu_hbm.at[e, :], wgu.at[pl.ds(p * pw, pw), pl.ds(bw, bw)]))
    first_local = len(pairs)
    for i in range(NZ):
        e = part_at(part_of(i - 2))
        pairs.append((act_hbm.at[:, e], base_f.at[:, pl.ds(i * pw, pw)]))
        pairs.append((grad_hbm.at[:, e], tok_b.at[own_rows, pl.ds(i * pw, pw)]))
    for p in range(4):
        pairs.append((wd_hbm.at[:, part_at(part_of(p))], wd.at[p, pl.ds(0, bw), :]))
    pairs.append((sg_hbm.at[:, y], sg.at[0]))
    pairs.append((su_hbm.at[:, y], su.at[0]))
    local = [pltpu.make_async_copy(s, d, local_sem.at[i]) for i, (s, d) in enumerate(pairs)]

    for copy in local:
        copy.start()
    barrier = pltpu.get_barrier_semaphore()
    peers = [at_z(s) for s in (1, -1, 2, -2)] + [at_y(s) for s in (1, -1, 2)]
    peers += [(p_next, k), (p_prev, k)]
    for to in peers:
        pl.semaphore_signal(barrier, inc=1, device_id=to, device_id_type=MESH)
    pl.semaphore_wait(barrier, len(peers))

    for which in range(3):
        for f in (1, 3, 0, 2):
            shared_weight(f, which).start()
    for copy in local[:first_local]:
        copy.wait()
    for d in (0, 1):
        weight_copy(d, 0).start()
        token_copy(0, d, 1).start()

    def pass_tokens(mb, step):
        for d in (0, 1):
            token_copy(mb, d, step).wait_recv()
            if step < STEPS:
                token_copy(mb, d, step + 1).start()

    def pass_weights(piece, onward):
        for d in (0, 1):
            weight_copy(d, piece).wait_recv()
            weight_copy(d, onward).start()

    def turn(j):
        return (y + j + j // 2 - 2 * (j // 3)) % NY

    def mask_at(mask, zb, j, owner, b):
        return mask[zb * NY + turn(j), (owner * NY + y) * blocks + b].astype(F32)

    def source(i):
        return (z + NZ + Z_REL[i]) % NZ

    def packed_at(owner):
        return pl.ds(aligned(owner * BLOCK, BLOCK), BLOCK)

    def pack(mask, zb, j, lanes, put):
        for i in range(NZ):
            owner = source(i)
            total = None
            for b in range(blocks):
                piece = acc[pl.ds(i * rows + b * BLOCK, BLOCK), lanes]
                piece = piece * mask_at(mask, zb, j, owner, b)
                total = piece if total is None else total + piece
            put(owner, total)

    def unpack(mask, zb, packed, w, put):
        @pl.loop(0, NY)
        def _(j):
            lanes = pl.ds(aligned(j * w, w), w)
            for i in range(NZ):
                owner = source(i)
                value = packed[packed_at(owner), lanes].astype(F32)
                for b in range(blocks):
                    on = mask_at(mask, zb, j, owner, b)
                    put(pl.ds(i * rows + b * BLOCK, BLOCK), lanes, (value * on).astype(BF16))

    helped = [(z + NZ + s) % NZ for s in FOREIGN]
    both = pl.ds(0, 2 * bw)

    def gates_for(j_from, j_to):
        @pl.loop(j_from, j_to)
        def _(j):
            lanes = pl.ds(aligned(j * 2 * bw, 2 * bw), 2 * bw)
            acc[:, both] = jnp.zeros((NZ * rows, 2 * bw), F32)

            @pl.loop(0, 4)
            def _(p):
                acc[:, both] += jnp.dot(
                    tok_f[:, pl.ds(aligned((p + 2) * pw, pw), pw)],
                    wgu[pl.ds(aligned(p * pw, pw), pw), lanes],
                    preferred_element_type=F32,
                )

            def put_own(owner, value):
                pk_own[packed_at(owner), lanes] = value

            pack(mask_f, z, j, both, put_own)
            for f in range(4):
                acc[:, both] = jnp.dot(
                    tok_f[:, pl.ds((FOREIGN_PLACE[f] + 2) * pw, pw)],
                    wgu[pl.ds((4 + f) * pw, pw), lanes],
                    preferred_element_type=F32,
                )

                def put(owner, value):
                    pk_send[f, packed_at(owner), lanes] = value.astype(BF16)

                pack(mask_f, helped[f], j, both, put)

    for f in range(4):
        for which in (0, 1):
            shared_weight(f, which).wait_recv()
    for d in (0, 1):
        weight_copy(d, 1).start()
    pass_weights(0, 2)
    for step in (1, 2, 3):
        pass_tokens(0, step)
    pass_weights(1, 3)
    for copy in local[first_local:]:
        copy.wait()
    for f in range(4):
        shared_weight(f, 2).wait_recv()
    for d in (0, 1):
        weight_copy(d, 4).start()
    pass_tokens(0, 4)
    for d in (0, 1):
        token_copy(1, d, 1).start()
    pass_tokens(0, 5)
    gates_for(0, 3)
    pass_tokens(1, 1)
    pass_tokens(1, 2)
    for d in (0, 1):
        weight_copy(d, 2).wait_recv()
        weight_copy(d, 3).wait_recv()
    gates_for(3, 4)
    for f in range(4):
        to_owner(pk_send, pk_recv, 0, f).start()
    pass_tokens(1, 3)
    for f in range(4):
        to_owner(pk_send, pk_recv, 0, f).wait_recv()
    for j in range(NY):
        sums = []
        for lanes in (pl.ds(2 * j * bw, bw), pl.ds((2 * j + 1) * bw, bw)):
            total = pk_own[:, lanes]
            for f in range(4):
                total = total + pk_recv[f, :, lanes].astype(F32)
            sums.append(total)
        hidp[:, pl.ds(j * bw, bw)] = (jnp.maximum(sums[0], 0.0) * sums[1]).astype(BF16)
    for f in range(4):
        to_helper(hidp, hid_recv, 1, f).start()
    pass_weights(4, 8)
    for d in (0, 1):
        weight_copy(d, 5).start()
    pass_tokens(1, 4)

    def put_hidden(i):
        def put(at, lanes, value):
            hid[i, at, lanes] = value

        return put

    unpack(mask_f, z, hidp, bw, put_hidden(0))
    for f in range(4):
        to_helper(hidp, hid_recv, 1, f).wait_recv()
        unpack(mask_f, helped[f], hid_recv.at[f], bw, put_hidden(1 + f))
    ghp[...] = jnp.zeros(ghp.shape, F32)
    for d in (0, 1):
        for step in range(1, STEPS + 1):
            token_copy(0, d, step).wait_send()

    n_part = part.shape[0]

    def grad_hidden(q):
        lo = q * qcols
        at = pl.ds(aligned(lo, qcols), qcols)

        def add(i, zb):
            @pl.loop(0, NY)
            def _(j):
                lanes = pl.ds(aligned(j * bw, bw), bw)

                def put(owner, value):
                    ghp[i, packed_at(owner), lanes] += value

                pack(mask_b, zb, j, lanes, put)

        acc[...] = jnp.zeros(acc.shape, F32)

        @pl.loop(0, 4)
        def _(p):
            mine = pl.ds(aligned((p + 2) * pw + lo, qcols), qcols)
            acc[...] += dot_last(tok_b[:, mine], wd[p, :, at])

        add(0, z)
        for f in range(4):
            mine = pl.ds(aligned((FOREIGN_PLACE[f] + 2) * pw + lo, qcols), qcols)
            acc[...] = dot_last(tok_b[:, mine], wd[4 + f, :, at])
            add(1 + f, helped[f])

    def grads_packed():
        @pl.loop(0, NY)
        def _(j):
            lanes = pl.ds(aligned(j * bw, bw), bw)
            for owner in range(NZ):
                at = pl.ds(owner * BLOCK, BLOCK)
                grad = ghp[0, at, lanes]
                for f in range(4):
                    grad = grad + gh_recv[f, at, lanes].astype(F32)
                gate = up = None
                for b in range(blocks):
                    on = mask_at(mask_b, z, j, owner, b)
                    in_block = pl.ds(b * BLOCK, BLOCK)
                    g = sg[j, owner, in_block, :].astype(F32) * on
                    u = su[j, owner, in_block, :].astype(F32) * on
                    gate = g if gate is None else gate + g
                    up = u if up is None else up + u
                gradp[at, pl.ds(aligned(2 * j * bw, bw), bw)] = jnp.where(
                    gate > 0, grad * up, 0.0
                ).astype(BF16)
                gradp[at, pl.ds(aligned((2 * j + 1) * bw, bw), bw)] = (
                    grad * jnp.maximum(gate, 0.0)
                ).astype(BF16)

    def put_grads(i):
        def put(at, lanes, value):
            tok_f[at, pl.ds(i * 2 * NY * bw + lanes.start, 2 * bw)] = value

        return put

    def side_work(t):
        for q in range(1, QUARTERS):

            @pl.when(t == 2 * q - 1)
            def _():
                pass_weights(4 + q, 8 + q)
                if q < QUARTERS - 1:
                    for d in (0, 1):
                        weight_copy(d, 5 + q).start()
                else:
                    for peer in range(3):
                        for which in (0, 1):
                            saved_copy(peer, which).start()

        for q in range(QUARTERS):

            @pl.when(t == 2 * q)
            def _():
                for d in (0, 1):
                    weight_copy(d, 8 + q).wait_recv()

        @pl.when(t == 3)
        def _():
            pass_tokens(1, 5)

        @pl.when((t >= 3) & (t < 7))
        def _():
            grad_hidden(t - 3)

        @pl.when(t == 6)
        def _():
            for f in range(4):
                gh_send[f] = ghp[1 + f].astype(BF16)
                to_owner(gh_send, gh_recv, 2, f).start()

        @pl.when(t == 7)
        def _():
            for peer in range(3):
                for which in (0, 1):
                    saved_copy(peer, which).wait_recv()
            for f in range(4):
                to_owner(gh_send, gh_recv, 2, f).wait_recv()
            grads_packed()
            for f in range(4):
                to_helper(gradp, grad_recv, 3, f).start()

        @pl.when(t == 8)
        def _():
            unpack(mask_b, z, gradp, 2 * bw, put_grads(0))
            for f in range(4):
                to_helper(gradp, grad_recv, 3, f).wait_recv()
                unpack(mask_b, helped[f], grad_recv.at[f], 2 * bw, put_grads(1 + f))

    def local_part(t):
        def put(p, value):
            part[t % n_part, :, pl.ds(p * cols, cols)] = value

        @pl.when(t < chunks)
        def _():
            at = pl.ds(aligned(t * cols, cols), cols)
            for p in range(4):
                total = jnp.dot(hid[0], wd[p, :, at], preferred_element_type=F32)
                for f in range(4):
                    if FOREIGN_PLACE[f] == p:
                        total = total + jnp.dot(
                            hid[1 + f], wd[4 + f, :, at], preferred_element_type=F32
                        )
                put(p, total)

        @pl.when((t >= chunks) & (t < 2 * chunks))
        def _():
            def grads(i):
                return tok_f[:, pl.ds(i * 2 * NY * bw, 2 * NY * bw)]

            def weights(i):
                return wgu[pl.ds(aligned(i * pw + (t - chunks) * cols, cols), cols), :]

            for p in range(4):
                total = dot_last(grads(0), weights(p))
                for f in range(4):
                    if FOREIGN_PLACE[f] == p:
                        total = total + dot_last(grads(1 + f), weights(4 + f))
                put(p, total)

    def ring_step(step, c):
        b = c % RING
        pb = c % n_part
        for d in (0, 1):
            if step > 1:
                ring_copy(d, step - 1, c).wait_recv()

            @pl.when(c >= RING)
            def _():
                ring_copy(d, step, c - RING).wait_send()

            ahead = (STEPS + 1 - step) * (1 if d == RIGHT else -1)
            at = pl.ds(slot_at(ahead) * rows, rows)
            s = sbufs[step - 1]
            r = rbufs[step - 2]

            def mine(first, n):
                return part[pb, at, pl.ds(first * cols, n * cols)]

            def came(first, n):
                return r[d, b, :, pl.ds(first * cols, n * cols)]

            def put(first, n, value):
                s[d, b, :, pl.ds(first * cols, n * cols)] = value.astype(BF16)

            if d == RIGHT:
                put(0, 1, mine(0, 1))
                n = min(step, 4) - 1
                if n:
                    put(1, n, mine(1, n) + came(0, n).astype(F32))
                if step == STEPS:
                    put(4, 1, came(3, 1))
            else:
                put(step - 1, 1, mine(3, 1))
                skip = 1 if step == STEPS else 0
                n = step - 1 - skip
                if n:
                    put(skip, n, mine(3 - n, n) + came(skip, n).astype(F32))
                if skip:
                    put(0, 1, came(0, 1))
            ring_copy(d, step, c).start()

    def finish(c):
        b = c % RING
        for d in (0, 1):
            ring_copy(d, STEPS, c).wait_recv()

        @pl.when(c >= RING)
        def _():
            for i in range(NZ):
                out_copy(0, (c - RING) % chunks, i).wait_send()

        for mb in (0, 1):

            @pl.when((c >= mb * chunks) & (c < (mb + 1) * chunks))
            def _():
                cc = c - mb * chunks
                base = base_f if mb == 0 else tok_b
                for i in range(NZ):
                    at = pl.ds(aligned(i * pw + cc * cols, cols), cols)
                    total = base[own_rows, at].astype(F32)
                    if i < 5:
                        total += rbufs[4][LEFT, b, :, pl.ds(i * cols, cols)].astype(F32)
                    if i > 2:
                        total += rbufs[4][RIGHT, b, :, pl.ds((i - 3) * cols, cols)].astype(F32)
                    if 2 <= i < 6:
                        total += part[c % n_part, own_rows, pl.ds((i - 2) * cols, cols)]
                    obuf[b, :, pl.ds(i * cols, cols)] = total.astype(BF16)
                    out_copy(mb, cc, i).start()

    total = 2 * chunks

    @pl.loop(0, total + STEPS)
    def _(t):
        side_work(t)
        local_part(t)
        for step in range(1, STEPS + 1):

            @pl.when((t >= step - 1) & (t < total + step - 1))
            def _():
                ring_step(step, t - (step - 1))

        @pl.when(t >= STEPS)
        def _():
            finish(t - STEPS)

    @pl.loop(total - RING, total)
    def _(c):
        for d in (0, 1):
            for step in range(1, STEPS + 1):
                ring_copy(d, step, c).wait_send()
        for i in range(NZ):
            out_copy(1, c - chunks, i).wait_send()

    for d in (0, 1):
        for step in range(1, STEPS + 1):
            token_copy(1, d, step).wait_send()
        for piece in range(12):
            weight_copy(d, piece).wait_send()
    for f in range(4):
        for which in range(3):
            shared_weight(f, which).wait_send()
        to_owner(pk_send, pk_recv, 0, f).wait_send()
        to_helper(hidp, hid_recv, 1, f).wait_send()
        to_owner(gh_send, gh_recv, 2, f).wait_send()
        to_helper(gradp, grad_recv, 3, f).wait_send()
    for peer in range(3):
        for which in (0, 1):
            saved_copy(peer, which).wait_send()

    @pl.loop(0, chunks)
    def _(c):
        for mb in (0, 1):
            for i in range(NZ):
                out_copy(mb, c, i).wait_recv()


def per_device(act_fwd, grad_in, w_gate, w_up, w_down, saved_gate, saved_up, mask_fwd, mask_bwd):
    rows, width = act_fwd.shape[1:]
    bw = w_gate.shape[2]
    chunks = 8
    pw = width // NZ
    cols = pw // chunks
    all_rows = NZ * rows
    packed = NZ * BLOCK
    by_owner = (NZ, NY, rows, bw)
    anywhere = pl.BlockSpec(memory_space=pl.ANY)
    scalars = pl.BlockSpec(memory_space=pltpu.SMEM)
    dma = pltpu.SemaphoreType.DMA
    out = jax.ShapeDtypeStruct((rows, width), BF16)
    ring = [pltpu.VMEM((2, RING, rows, n * cols), BF16) for n in range(1, STEPS + 1)]
    ahead, behind = pl.pallas_call(
        functools.partial(kernel, chunks),
        out_shape=(out, out),
        in_specs=[anywhere] * 7 + [scalars] * 2,
        out_specs=(anywhere, anywhere),
        scratch_shapes=[
            pltpu.VMEM((all_rows, width), BF16),
            pltpu.VMEM((all_rows, width), BF16),
            pltpu.VMEM((width, NY * 2 * bw), BF16),
            pltpu.VMEM((NZ, NY * bw, pw), BF16),
            pltpu.VMEM((NY, NZ, rows, bw), BF16),
            pltpu.VMEM((NY, NZ, rows, bw), BF16),
            pltpu.VMEM((5, all_rows, NY * bw), BF16),
            pltpu.VMEM((all_rows, NY * bw), F32),
            pltpu.VMEM((rows, width), BF16),
            pltpu.VMEM((packed, NY * 2 * bw), F32),
            pltpu.VMEM((4, packed, NY * 2 * bw), BF16),
            pltpu.VMEM((4, packed, NY * 2 * bw), BF16),
            pltpu.VMEM((packed, NY * bw), BF16),
            pltpu.VMEM((4, packed, NY * bw), BF16),
            pltpu.VMEM((5, packed, NY * bw), F32),
            pltpu.VMEM((4, packed, NY * bw), BF16),
            pltpu.VMEM((4, packed, NY * bw), BF16),
            pltpu.VMEM((packed, NY * 2 * bw), BF16),
            pltpu.VMEM((4, packed, NY * 2 * bw), BF16),
            pltpu.VMEM((STEPS + 1, all_rows, 4 * cols), F32),
            pltpu.VMEM((RING, rows, NZ * cols), BF16),
            *ring,
            *ring,
            dma((38,)),
            dma((2, 2, STEPS)),
            dma((2, 2, STEPS)),
            dma((4, 3)),
            dma((4, 3)),
            dma((2, 12)),
            dma((2, 12)),
            dma((3, 2)),
            dma((3, 2)),
            dma((4, 4)),
            dma((4, 4)),
            dma((2, STEPS, RING)),
            dma((2, STEPS, RING)),
            dma((RING, NZ)),
            dma((2, chunks, NZ)),
        ],
        compiler_params=pltpu.CompilerParams(
            collective_id=0, has_side_effects=True, vmem_limit_bytes=67043328
        ),
    )(
        act_fwd[0],
        grad_in[0],
        w_gate[0],
        w_up[0],
        w_down[0],
        saved_gate[0].reshape(by_owner),
        saved_up[0].reshape(by_owner),
        mask_fwd[0].T,
        mask_bwd[0].T,
    )
    return ahead[None], behind[None]


def solution(mesh):
    in_specs = (
        P("pipe", "bundle", None),
        P("pipe", "bundle", None),
        P("pipe", None, "bundle"),
        P("pipe", None, "bundle"),
        P("pipe", "bundle", None),
        P("pipe", None, "bundle"),
        P("pipe", None, "bundle"),
        P("pipe", None, None),
        P("pipe", None, None),
    )
    out_specs = (P("pipe", "bundle", None), P("pipe", "bundle", None))
    return jax.shard_map(
        per_device, mesh=mesh, in_specs=in_specs, out_specs=out_specs, check_vma=False
    )
```

```python
import functools

import jax
import jax.numpy as jnp
from jax import lax
from jax.experimental import pallas as pl
from jax.experimental.pallas import tpu as pltpu
from jax.sharding import PartitionSpec as P

MESH = pl.DeviceIdType.MESH
F32, BF16 = jnp.float32, jnp.bfloat16
NZ, NY = 8, 4
BLOCK = 16
Z_REL = (0, 1, -1, 2, -2, 3, -3, 4)
RIGHT, LEFT = 0, 1
RING = 4
QUARTERS = 4
STEPS = 5
FOREIGN = (-1, -2, 1, 2)
FOREIGN_PLACE = (0, 0, 3, 3)
AWAY = (-1, -1, 1, 1)


def slot_at(rel):
    rel = (rel + 3) % NZ - 3
    return Z_REL.index(rel)


def aligned(x, n):
    return pl.multiple_of(x, n)


def dot_last(a, b):
    return lax.dot_general(a, b, (((1,), (1,)), ((), ())), preferred_element_type=F32)


def kernel(chunks, *refs):
    (act_hbm, grad_hbm, wg_hbm, wu_hbm, wd_hbm, sg_hbm, su_hbm, mask_f, mask_b) = refs[:9]
    out_f, out_b = refs[9:11]
    (tok_f, tok_b, wgu, wd, sg, su, hid, acc, base_f) = refs[11:20]
    (pk_own, pk_send, pk_recv, hidp, hid_recv) = refs[20:25]
    (ghp, gh_send, gh_recv, gradp, grad_recv) = refs[25:30]
    part, obuf = refs[30:32]
    sbufs, rbufs = refs[32:37], refs[37:42]
    (local_sem, z_send, z_recv, w_send, w_recv, y_send, y_recv, s_send, s_recv) = refs[42:51]
    (x_send, x_recv, r_send, r_recv, o_send, o_recv) = refs[51:57]

    rows, width = act_hbm.shape
    bw = wg_hbm.shape[1]
    pw = width // NZ
    blocks = rows // BLOCK
    n_pipe = lax.axis_size("pipe")
    pipe = lax.axis_index("pipe")
    k = lax.axis_index("bundle")
    z, y = k // NY, k % NY

    def at_z(step):
        return (pipe, ((z + NZ + step) % NZ) * NY + y)

    def at_y(step):
        return (pipe, z * NY + (y + NY + step) % NY)

    p_next = (pipe + 1) % n_pipe
    p_prev = (pipe + n_pipe - 1) % n_pipe
    z_to = (at_z(1), at_z(-1))
    y_to = (at_y(1), at_y(-1))
    toks = (tok_f, tok_b)
    cols = pw // chunks
    qcols = pw // QUARTERS

    def remote(src, dst, send, recv, to):
        return pltpu.make_async_remote_copy(
            src_ref=src,
            dst_ref=dst,
            send_sem=send,
            recv_sem=recv,
            device_id=to,
            device_id_type=MESH,
        )

    def part_of(place):
        return (z + 2 * NZ - place) % NZ

    def part_at(e):
        return pl.ds(aligned(e * pw, pw), pw)

    def token_copy(mb, d, step):
        tok = toks[mb]
        n = (STEPS + 1 - step) * pw
        sign = -1 if d == RIGHT else 1
        first, then = ((step - 1) * pw, step * pw) if d == RIGHT else (3 * pw, 2 * pw)
        src = tok.at[pl.ds(slot_at(sign * (step - 1)) * rows, rows), pl.ds(first, n)]
        dst = tok.at[pl.ds(slot_at(sign * step) * rows, rows), pl.ds(then, n)]
        at = (mb, d, step - 1)
        return remote(src, dst, z_send.at[at], z_recv.at[at], z_to[d])

    def shared_weight(f, which):
        e = (z + NZ + (1, 2, -4, -5)[f]) % NZ
        to = at_z((1, 2, -1, -2)[f])
        if which < 2:
            src = (wg_hbm, wu_hbm)[which].at[part_at(e), :]
            dst = wgu.at[pl.ds((4 + f) * pw, pw), pl.ds(which * bw, bw)]
        else:
            src = wd_hbm.at[:, part_at(e)]
            dst = wd.at[4 + f, pl.ds(0, bw), :]
        return remote(src, dst, w_send.at[f, which], w_recv.at[f, which], to)

    def weight_copy(d, piece):
        j = 2 if d == RIGHT else 1
        half = 2 * pw
        if piece < 2:
            at = pl.ds(piece * 4 * pw, 4 * pw)
            src = wgu.at[at, pl.ds(0, 2 * bw)]
            dst = wgu.at[at, pl.ds(j * 2 * bw, 2 * bw)]
        elif piece < 4:
            at = pl.ds((piece - 2) * 4 * pw + d * half, half)
            src = wgu.at[at, pl.ds(j * 2 * bw, 2 * bw)]
            dst = wgu.at[at, pl.ds(3 * 2 * bw, 2 * bw)]
        elif piece < 8:
            at = pl.ds((piece - 4) * qcols, qcols)
            src = wd.at[:, pl.ds(0, bw), at]
            dst = wd.at[:, pl.ds(j * bw, bw), at]
        else:
            at = pl.ds((piece - 8) * qcols, qcols)
            hb = bw // 2
            src = wd.at[:, pl.ds(j * bw + d * hb, hb), at]
            dst = wd.at[:, pl.ds(3 * bw + d * hb, hb), at]
        return remote(src, dst, y_send.at[d, piece], y_recv.at[d, piece], y_to[d])

    def saved_copy(peer, which):
        step = (1, -1, 2)[peer]
        src = (sg_hbm, su_hbm)[which].at[:, (y + NY + step) % NY]
        dst = (sg, su)[which].at[(2, 1, 3)[peer]]
        at = (peer, which)
        return remote(src, dst, s_send.at[at], s_recv.at[at], at_y(step))

    def to_owner(src, dst, kind, f):
        return remote(
            src.at[f], dst.at[f], x_send.at[kind, f], x_recv.at[kind, f], at_z(AWAY[f])
        )

    def to_helper(src, dst, kind, f):
        src = dst.at[f - 1] if f % 2 else src
        return remote(
            src, dst.at[f], x_send.at[kind, f], x_recv.at[kind, f], at_z(-AWAY[f])
        )

    def start_owner(src, dst, kind):
        for f in (1, 3):
            to_owner(src, dst, kind, f).start()

    def join_owner(src, dst, kind):
        for f in (1, 3):
            to_owner(src, dst, kind, f).wait_recv()
            src[f - 1] = (src[f - 1].astype(F32) + dst[f].astype(F32)).astype(BF16)
            to_owner(src, dst, kind, f - 1).start()

    def start_helpers(src, dst, kind):
        for f in (0, 2):
            to_helper(src, dst, kind, f).start()

    def pass_helpers(src, dst, kind):
        for f in (0, 2):
            to_helper(src, dst, kind, f).wait_recv()
            to_helper(src, dst, kind, f + 1).start()

    def ring_copy(d, step, c):
        b = c % RING
        return remote(
            sbufs[step - 1].at[d, b],
            rbufs[step - 1].at[d, b],
            r_send.at[d, step - 1, b],
            r_recv.at[d, step - 1, b],
            z_to[d],
        )

    def out_copy(mb, c, i):
        e = part_of(i - 2)
        to = (p_next, k) if mb == 0 else (p_prev, k)
        return remote(
            obuf.at[c % RING, :, pl.ds(i * cols, cols)],
            (out_f, out_b)[mb].at[:, pl.ds(aligned(e * pw + c * cols, cols), cols)],
            o_send.at[c % RING, i],
            o_recv.at[mb, c, i],
            to,
        )

    own_rows = pl.ds(0, rows)
    pairs = []
    for i in range(NZ):
        pairs.append(
            (act_hbm.at[:, part_at(part_of(i - 2))], tok_f.at[own_rows, pl.ds(i * pw, pw)])
        )
    for p in range(4):
        e = part_at(part_of(p))
        pairs.append((wg_hbm.at[e, :], wgu.at[pl.ds(p * pw, pw), pl.ds(0, bw)]))
        pairs.append((wu_hbm.at[e, :], wgu.at[pl.ds(p * pw, pw), pl.ds(bw, bw)]))
    first_local = len(pairs)
    for i in range(NZ):
        e = part_at(part_of(i - 2))
        pairs.append((act_hbm.at[:, e], base_f.at[:, pl.ds(i * pw, pw)]))
        pairs.append((grad_hbm.at[:, e], tok_b.at[own_rows, pl.ds(i * pw, pw)]))
    for p in range(4):
        pairs.append((wd_hbm.at[:, part_at(part_of(p))], wd.at[p, pl.ds(0, bw), :]))
    pairs.append((sg_hbm.at[:, y], sg.at[0]))
    pairs.append((su_hbm.at[:, y], su.at[0]))
    local = [pltpu.make_async_copy(s, d, local_sem.at[i]) for i, (s, d) in enumerate(pairs)]

    for copy in local:
        copy.start()
    barrier = pltpu.get_barrier_semaphore()
    peers = [at_z(s) for s in (1, -1, 2, -2)] + [at_y(s) for s in (1, -1, 2)]
    peers += [(p_next, k), (p_prev, k)]
    for to in peers:
        pl.semaphore_signal(barrier, inc=1, device_id=to, device_id_type=MESH)
    pl.semaphore_wait(barrier, len(peers))

    for which in range(3):
        for f in (1, 3, 0, 2):
            shared_weight(f, which).start()
    for copy in local[:first_local]:
        copy.wait()
    for d in (0, 1):
        weight_copy(d, 0).start()
        token_copy(0, d, 1).start()

    def pass_tokens(mb, step):
        for d in (0, 1):
            token_copy(mb, d, step).wait_recv()
            if step < STEPS:
                token_copy(mb, d, step + 1).start()

    def pass_weights(piece, onward):
        for d in (0, 1):
            weight_copy(d, piece).wait_recv()
            weight_copy(d, onward).start()

    def turn(j):
        return (y + j + j // 2 - 2 * (j // 3)) % NY

    def mask_at(mask, zb, j, owner, b):
        return mask[zb * NY + turn(j), (owner * NY + y) * blocks + b].astype(F32)

    def source(i):
        return (z + NZ + Z_REL[i]) % NZ

    def packed_at(owner):
        return pl.ds(aligned(owner * BLOCK, BLOCK), BLOCK)

    def pack(mask, zb, j, lanes, put):
        for i in range(NZ):
            owner = source(i)
            total = None
            for b in range(blocks):
                piece = acc[pl.ds(i * rows + b * BLOCK, BLOCK), lanes]
                piece = piece * mask_at(mask, zb, j, owner, b)
                total = piece if total is None else total + piece
            put(owner, total)

    def unpack(mask, zb, packed, w, put):
        @pl.loop(0, NY)
        def _(j):
            lanes = pl.ds(aligned(j * w, w), w)
            for i in range(NZ):
                owner = source(i)
                value = packed[packed_at(owner), lanes].astype(F32)
                for b in range(blocks):
                    on = mask_at(mask, zb, j, owner, b)
                    put(pl.ds(i * rows + b * BLOCK, BLOCK), lanes, (value * on).astype(BF16))

    helped = [(z + NZ + s) % NZ for s in FOREIGN]
    both = pl.ds(0, 2 * bw)

    def gates_for(j_from, j_to):
        @pl.loop(j_from, j_to)
        def _(j):
            lanes = pl.ds(aligned(j * 2 * bw, 2 * bw), 2 * bw)
            acc[:, both] = jnp.zeros((NZ * rows, 2 * bw), F32)

            @pl.loop(0, 4)
            def _(p):
                acc[:, both] += jnp.dot(
                    tok_f[:, pl.ds(aligned((p + 2) * pw, pw), pw)],
                    wgu[pl.ds(aligned(p * pw, pw), pw), lanes],
                    preferred_element_type=F32,
                )

            def put_own(owner, value):
                pk_own[packed_at(owner), lanes] = value

            pack(mask_f, z, j, both, put_own)
            for f in range(4):
                acc[:, both] = jnp.dot(
                    tok_f[:, pl.ds((FOREIGN_PLACE[f] + 2) * pw, pw)],
                    wgu[pl.ds((4 + f) * pw, pw), lanes],
                    preferred_element_type=F32,
                )

                def put(owner, value):
                    pk_send[f, packed_at(owner), lanes] = value.astype(BF16)

                pack(mask_f, helped[f], j, both, put)

    for f in range(4):
        for which in (0, 1):
            shared_weight(f, which).wait_recv()
    for d in (0, 1):
        weight_copy(d, 1).start()
    pass_weights(0, 2)
    for step in (1, 2, 3):
        pass_tokens(0, step)
    pass_weights(1, 3)
    for copy in local[first_local:]:
        copy.wait()
    for f in range(4):
        shared_weight(f, 2).wait_recv()
    for d in (0, 1):
        weight_copy(d, 4).start()
    pass_tokens(0, 4)
    for d in (0, 1):
        token_copy(1, d, 1).start()
    pass_tokens(0, 5)
    gates_for(0, 3)
    pass_tokens(1, 1)
    pass_tokens(1, 2)
    for d in (0, 1):
        weight_copy(d, 2).wait_recv()
        weight_copy(d, 3).wait_recv()
    gates_for(3, 4)
    start_owner(pk_send, pk_recv, 0)
    pass_tokens(1, 3)
    join_owner(pk_send, pk_recv, 0)
    pass_weights(4, 8)
    for d in (0, 1):
        weight_copy(d, 5).start()
    for f in (0, 2):
        to_owner(pk_send, pk_recv, 0, f).wait_recv()
    for j in range(NY):
        sums = []
        for lanes in (pl.ds(2 * j * bw, bw), pl.ds((2 * j + 1) * bw, bw)):
            total = pk_own[:, lanes]
            for f in (0, 2):
                total = total + pk_recv[f, :, lanes].astype(F32)
            sums.append(total)
        hidp[:, pl.ds(j * bw, bw)] = (jnp.maximum(sums[0], 0.0) * sums[1]).astype(BF16)
    start_helpers(hidp, hid_recv, 1)
    pass_tokens(1, 4)

    def put_hidden(i):
        def put(at, lanes, value):
            hid[i, at, lanes] = value

        return put

    unpack(mask_f, z, hidp, bw, put_hidden(0))
    pass_helpers(hidp, hid_recv, 1)
    for f in (0, 2, 1, 3):
        if f % 2:
            to_helper(hidp, hid_recv, 1, f).wait_recv()
        unpack(mask_f, helped[f], hid_recv.at[f], bw, put_hidden(1 + f))
    ghp[...] = jnp.zeros(ghp.shape, F32)
    for d in (0, 1):
        for step in range(1, STEPS + 1):
            token_copy(0, d, step).wait_send()

    n_part = part.shape[0]

    def grad_hidden(q):
        lo = q * qcols
        at = pl.ds(aligned(lo, qcols), qcols)

        def add(i, zb):
            @pl.loop(0, NY)
            def _(j):
                lanes = pl.ds(aligned(j * bw, bw), bw)

                def put(owner, value):
                    ghp[i, packed_at(owner), lanes] += value

                pack(mask_b, zb, j, lanes, put)

        acc[...] = jnp.zeros(acc.shape, F32)

        @pl.loop(0, 4)
        def _(p):
            mine = pl.ds(aligned((p + 2) * pw + lo, qcols), qcols)
            acc[...] += dot_last(tok_b[:, mine], wd[p, :, at])

        add(0, z)
        for f in range(4):
            mine = pl.ds(aligned((FOREIGN_PLACE[f] + 2) * pw + lo, qcols), qcols)
            acc[...] = dot_last(tok_b[:, mine], wd[4 + f, :, at])
            add(1 + f, helped[f])

    def grads_packed():
        @pl.loop(0, NY)
        def _(j):
            lanes = pl.ds(aligned(j * bw, bw), bw)
            for owner in range(NZ):
                at = pl.ds(owner * BLOCK, BLOCK)
                grad = ghp[0, at, lanes]
                for f in (0, 2):
                    grad = grad + gh_recv[f, at, lanes].astype(F32)
                gate = up = None
                for b in range(blocks):
                    on = mask_at(mask_b, z, j, owner, b)
                    in_block = pl.ds(b * BLOCK, BLOCK)
                    g = sg[j, owner, in_block, :].astype(F32) * on
                    u = su[j, owner, in_block, :].astype(F32) * on
                    gate = g if gate is None else gate + g
                    up = u if up is None else up + u
                gradp[at, pl.ds(aligned(2 * j * bw, bw), bw)] = jnp.where(
                    gate > 0, grad * up, 0.0
                ).astype(BF16)
                gradp[at, pl.ds(aligned((2 * j + 1) * bw, bw), bw)] = (
                    grad * jnp.maximum(gate, 0.0)
                ).astype(BF16)

    def put_grads(i):
        def put(at, lanes, value):
            tok_f[at, pl.ds(i * 2 * NY * bw + lanes.start, 2 * bw)] = value

        return put

    def side_work(t):
        for q in range(1, QUARTERS):

            @pl.when(t == 2 * q - 1)
            def _():
                pass_weights(4 + q, 8 + q)
                if q < QUARTERS - 1:
                    for d in (0, 1):
                        weight_copy(d, 5 + q).start()
                else:
                    for peer in range(3):
                        for which in (0, 1):
                            saved_copy(peer, which).start()

        for q in range(QUARTERS):

            @pl.when(t == 2 * q)
            def _():
                for d in (0, 1):
                    weight_copy(d, 8 + q).wait_recv()

        @pl.when(t == 3)
        def _():
            pass_tokens(1, 5)

        @pl.when((t >= 3) & (t < 7))
        def _():
            grad_hidden(t - 3)

        @pl.when(t == 6)
        def _():
            for f in range(4):
                gh_send[f] = ghp[1 + f].astype(BF16)
            start_owner(gh_send, gh_recv, 2)

        @pl.when(t == 7)
        def _():
            for peer in range(3):
                for which in (0, 1):
                    saved_copy(peer, which).wait_recv()
            for f in (0, 2):
                to_owner(gh_send, gh_recv, 2, f).wait_recv()
            grads_packed()
            start_helpers(gradp, grad_recv, 3)

        @pl.when(t == 8)
        def _():
            unpack(mask_b, z, gradp, 2 * bw, put_grads(0))
            for f in (0, 2, 1, 3):
                if f % 2:
                    to_helper(gradp, grad_recv, 3, f).wait_recv()
                unpack(mask_b, helped[f], grad_recv.at[f], 2 * bw, put_grads(1 + f))

    def local_part(t):
        def put(p, value):
            part[t % n_part, :, pl.ds(p * cols, cols)] = value

        @pl.when(t < chunks)
        def _():
            at = pl.ds(aligned(t * cols, cols), cols)
            for p in range(4):
                total = jnp.dot(hid[0], wd[p, :, at], preferred_element_type=F32)
                for f in range(4):
                    if FOREIGN_PLACE[f] == p:
                        total = total + jnp.dot(
                            hid[1 + f], wd[4 + f, :, at], preferred_element_type=F32
                        )
                put(p, total)

        @pl.when((t >= chunks) & (t < 2 * chunks))
        def _():
            def grads(i):
                return tok_f[:, pl.ds(i * 2 * NY * bw, 2 * NY * bw)]

            def weights(i):
                return wgu[pl.ds(aligned(i * pw + (t - chunks) * cols, cols), cols), :]

            for p in range(4):
                total = dot_last(grads(0), weights(p))
                for f in range(4):
                    if FOREIGN_PLACE[f] == p:
                        total = total + dot_last(grads(1 + f), weights(4 + f))
                put(p, total)

    def ring_step(step, c):
        b = c % RING
        pb = c % n_part
        for d in (0, 1):
            if step > 1:
                ring_copy(d, step - 1, c).wait_recv()

            @pl.when(c >= RING)
            def _():
                ring_copy(d, step, c - RING).wait_send()

            ahead = (STEPS + 1 - step) * (1 if d == RIGHT else -1)
            at = pl.ds(slot_at(ahead) * rows, rows)
            s = sbufs[step - 1]
            r = rbufs[step - 2]

            def mine(first, n):
                return part[pb, at, pl.ds(first * cols, n * cols)]

            def came(first, n):
                return r[d, b, :, pl.ds(first * cols, n * cols)]

            def put(first, n, value):
                s[d, b, :, pl.ds(first * cols, n * cols)] = value.astype(BF16)

            if d == RIGHT:
                put(0, 1, mine(0, 1))
                n = min(step, 4) - 1
                if n:
                    put(1, n, mine(1, n) + came(0, n).astype(F32))
                if step == STEPS:
                    put(4, 1, came(3, 1))
            else:
                put(step - 1, 1, mine(3, 1))
                skip = 1 if step == STEPS else 0
                n = step - 1 - skip
                if n:
                    put(skip, n, mine(3 - n, n) + came(skip, n).astype(F32))
                if skip:
                    put(0, 1, came(0, 1))
            ring_copy(d, step, c).start()

    def finish(c):
        b = c % RING
        for d in (0, 1):
            ring_copy(d, STEPS, c).wait_recv()

        @pl.when(c >= RING)
        def _():
            for i in range(NZ):
                out_copy(0, (c - RING) % chunks, i).wait_send()

        for mb in (0, 1):

            @pl.when((c >= mb * chunks) & (c < (mb + 1) * chunks))
            def _():
                cc = c - mb * chunks
                base = base_f if mb == 0 else tok_b
                for i in range(NZ):
                    at = pl.ds(aligned(i * pw + cc * cols, cols), cols)
                    total = base[own_rows, at].astype(F32)
                    if i < 5:
                        total += rbufs[4][LEFT, b, :, pl.ds(i * cols, cols)].astype(F32)
                    if i > 2:
                        total += rbufs[4][RIGHT, b, :, pl.ds((i - 3) * cols, cols)].astype(F32)
                    if 2 <= i < 6:
                        total += part[c % n_part, own_rows, pl.ds((i - 2) * cols, cols)]
                    obuf[b, :, pl.ds(i * cols, cols)] = total.astype(BF16)
                    out_copy(mb, cc, i).start()

    total = 2 * chunks

    @pl.loop(0, total + STEPS)
    def _(t):
        side_work(t)
        local_part(t)
        for step in range(1, STEPS + 1):

            @pl.when((t >= step - 1) & (t < total + step - 1))
            def _():
                ring_step(step, t - (step - 1))

        @pl.when(t >= STEPS)
        def _():
            finish(t - STEPS)

        @pl.when(t == chunks - 2)
        def _():
            join_owner(gh_send, gh_recv, 2)

        @pl.when(t == chunks - 1)
        def _():
            pass_helpers(gradp, grad_recv, 3)

    @pl.loop(total - RING, total)
    def _(c):
        for d in (0, 1):
            for step in range(1, STEPS + 1):
                ring_copy(d, step, c).wait_send()
        for i in range(NZ):
            out_copy(1, c - chunks, i).wait_send()

    for d in (0, 1):
        for step in range(1, STEPS + 1):
            token_copy(1, d, step).wait_send()
        for piece in range(12):
            weight_copy(d, piece).wait_send()
    for f in range(4):
        for which in range(3):
            shared_weight(f, which).wait_send()
        to_owner(pk_send, pk_recv, 0, f).wait_send()
        to_helper(hidp, hid_recv, 1, f).wait_send()
        to_owner(gh_send, gh_recv, 2, f).wait_send()
        to_helper(gradp, grad_recv, 3, f).wait_send()
    for peer in range(3):
        for which in (0, 1):
            saved_copy(peer, which).wait_send()

    @pl.loop(0, chunks)
    def _(c):
        for mb in (0, 1):
            for i in range(NZ):
                out_copy(mb, c, i).wait_recv()


def per_device(act_fwd, grad_in, w_gate, w_up, w_down, saved_gate, saved_up, mask_fwd, mask_bwd):
    rows, width = act_fwd.shape[1:]
    bw = w_gate.shape[2]
    chunks = 8
    pw = width // NZ
    cols = pw // chunks
    all_rows = NZ * rows
    packed = NZ * BLOCK
    by_owner = (NZ, NY, rows, bw)
    anywhere = pl.BlockSpec(memory_space=pl.ANY)
    scalars = pl.BlockSpec(memory_space=pltpu.SMEM)
    dma = pltpu.SemaphoreType.DMA
    out = jax.ShapeDtypeStruct((rows, width), BF16)
    ring = [pltpu.VMEM((2, RING, rows, n * cols), BF16) for n in range(1, STEPS + 1)]
    ahead, behind = pl.pallas_call(
        functools.partial(kernel, chunks),
        out_shape=(out, out),
        in_specs=[anywhere] * 7 + [scalars] * 2,
        out_specs=(anywhere, anywhere),
        scratch_shapes=[
            pltpu.VMEM((all_rows, width), BF16),
            pltpu.VMEM((all_rows, width), BF16),
            pltpu.VMEM((width, NY * 2 * bw), BF16),
            pltpu.VMEM((NZ, NY * bw, pw), BF16),
            pltpu.VMEM((NY, NZ, rows, bw), BF16),
            pltpu.VMEM((NY, NZ, rows, bw), BF16),
            pltpu.VMEM((5, all_rows, NY * bw), BF16),
            pltpu.VMEM((all_rows, NY * bw), F32),
            pltpu.VMEM((rows, width), BF16),
            pltpu.VMEM((packed, NY * 2 * bw), F32),
            pltpu.VMEM((4, packed, NY * 2 * bw), BF16),
            pltpu.VMEM((4, packed, NY * 2 * bw), BF16),
            pltpu.VMEM((packed, NY * bw), BF16),
            pltpu.VMEM((4, packed, NY * bw), BF16),
            pltpu.VMEM((5, packed, NY * bw), F32),
            pltpu.VMEM((4, packed, NY * bw), BF16),
            pltpu.VMEM((4, packed, NY * bw), BF16),
            pltpu.VMEM((packed, NY * 2 * bw), BF16),
            pltpu.VMEM((4, packed, NY * 2 * bw), BF16),
            pltpu.VMEM((STEPS + 1, all_rows, 4 * cols), F32),
            pltpu.VMEM((RING, rows, NZ * cols), BF16),
            *ring,
            *ring,
            dma((38,)),
            dma((2, 2, STEPS)),
            dma((2, 2, STEPS)),
            dma((4, 3)),
            dma((4, 3)),
            dma((2, 12)),
            dma((2, 12)),
            dma((3, 2)),
            dma((3, 2)),
            dma((4, 4)),
            dma((4, 4)),
            dma((2, STEPS, RING)),
            dma((2, STEPS, RING)),
            dma((RING, NZ)),
            dma((2, chunks, NZ)),
        ],
        compiler_params=pltpu.CompilerParams(
            collective_id=0, has_side_effects=True, vmem_limit_bytes=67043328
        ),
    )(
        act_fwd[0],
        grad_in[0],
        w_gate[0],
        w_up[0],
        w_down[0],
        saved_gate[0].reshape(by_owner),
        saved_up[0].reshape(by_owner),
        mask_fwd[0].T,
        mask_bwd[0].T,
    )
    return ahead[None], behind[None]


def solution(mesh):
    in_specs = (
        P("pipe", "bundle", None),
        P("pipe", "bundle", None),
        P("pipe", None, "bundle"),
        P("pipe", None, "bundle"),
        P("pipe", "bundle", None),
        P("pipe", None, "bundle"),
        P("pipe", None, "bundle"),
        P("pipe", None, None),
        P("pipe", None, None),
    )
    out_specs = (P("pipe", "bundle", None), P("pipe", "bundle", None))
    return jax.shard_map(
        per_device, mesh=mesh, in_specs=in_specs, out_specs=out_specs, check_vma=False
    )
```
